32 devices in a mesh: sub: 2 (over x), chan: 8 (over z, y), seg: 2 (over core).
Axes of the slice: x: 2, y: 2, z: 4, core: 2. Of those that a mesh axis runs over, the one named last changes fastest.
Arguments:
- raw: bfloat16 [2048, 65536], P(('sub', 'chan'), 'seg'), parts along dimension 0, may hold values from -120 to 120, as said below
- seg_mask: int32 [2048, 4], P(('sub', 'chan')), parts along dimension 0, may hold values 0 or 1
- band: int32 [2048, 2], P(('sub', 'chan')), parts along dimension 0, may hold values from 1 to 256, as said below
Outputs:
- correlations: bfloat16 [2048, 401, 512], P(('sub', 'chan'), None, 'seg'), parts along dimension 0
The draws below stay inside these ranges and needn't reach their ends.
There are 2 independent parts, one for each index of `sub`. The reference program is written for one: setup_inputs(seed, part) draws one part's arguments, and reference() takes and returns one part's arrays. A program takes and returns all parts, laid end to end along the dimension named above; each array names one. Nothing has to cross between parts.
Inputs may be any that keep to these rules, and one draw needn't show every extreme that they name: raw holds independent colored noise of a different amplitude for each channel and segment. band[i, 0] lies in 1 to 32 and band[i, 1] in 225 to 256.
All inputs are finite; a program needn't handle non-finite values. No bound on the sum of `seg_mask` on one device may be relied on, other than what follows from the above.
Results may differ from the reference program's by a relative error of at most 0.0081.
Values may be sent and summed in bfloat16 or wider, within the bound.
A program may use at most 256 MiB of HBM per device.

```python
import math
import jax
import jax.numpy as jnp
from jax import lax

C = 1024
W = 512
K = 128
MAXLAG = 200
R = 4
WSEG = 32
SEGS = 4
N_CHAN = 8


def draw_raw(key, part):
    key_noise, key_scale, key_color = jax.random.split(jax.random.fold_in(key, 11), 3)
    length = WSEG * W
    noise = jnp.clip(jax.random.normal(key_noise, (C, SEGS, length + 1), jnp.float32), -6.0, 6.0)
    amplitude = jnp.exp(jax.random.uniform(key_scale, (C, SEGS, 1), jnp.float32) * math.log(10.0))
    color = jax.random.uniform(key_color, (C, SEGS, 1), jnp.float32, -0.8, 0.8)
    series = amplitude * (noise[:, :, 1:] + color * noise[:, :, :-1])
    return series.reshape(C, SEGS * length).astype(jnp.bfloat16)


def draw_band(key, part):
    key_low, key_high = jax.random.split(jax.random.fold_in(key, 7))
    lower_limit = jax.random.randint(key_low, (C,), 1, 1 + C // 32, dtype=jnp.int32)
    upper_limit = C // 4 - jax.random.randint(key_high, (C,), 0, C // 32, dtype=jnp.int32)
    lower_limit = lower_limit.at[0].set(1)
    upper_limit = upper_limit.at[0].set(C // 4)
    return jnp.stack([lower_limit, upper_limit], axis=1)


def plant(values, own_key, smallest, largest):
    longest = values.shape.index(max(values.shape))
    spots = []
    for shift in (0, 1):
        where = [jax.random.randint(jax.random.fold_in(own_key, axis), (), 0, length) for axis, length in enumerate(values.shape)]
        where[longest] = (where[longest] + shift) % values.shape[longest]
        spots.append(tuple(where))
    return values.at[spots[0]].set(smallest).at[spots[1]].set(largest)


def setup_inputs(seed: int = 0, part: int = 0) -> dict:
    key_of = jax.random.split(jax.random.key(seed), 4)
    own_keys = jax.random.split(jax.random.fold_in(key_of[3], part), 4)
    return {
        "raw": draw_raw(jax.random.fold_in(jax.random.fold_in(key_of[3], part), 71), part),
        "seg_mask": plant((jax.random.randint(own_keys[1], (C, SEGS), 0, 4) < 3).astype(jnp.int32), jax.random.fold_in(own_keys[1], 1), 0, 1),
        "band": draw_band(jax.random.fold_in(jax.random.fold_in(key_of[3], part), 71), part),
    }


EPSILON = 1e-06

def transform_table(length, bins):
    samples = jnp.arange(length, dtype=jnp.float32)
    freqs = jnp.arange(1, bins + 1, dtype=jnp.float32)
    phase = 2.0 * math.pi * samples[:, None] * freqs[None, :] / length
    taper = 0.5 - 0.5 * jnp.cos(2.0 * math.pi * samples / length)
    weight = taper[:, None] / math.sqrt(length)
    return jnp.concatenate([weight * jnp.cos(phase), -weight * jnp.sin(phase)], axis=1).astype(jnp.bfloat16)

def lag_table(length, bins, reach):
    shifts = jnp.arange(-reach, reach + 1, dtype=jnp.float32)
    freqs = jnp.arange(1, bins + 1, dtype=jnp.float32)
    phase = 2.0 * math.pi * shifts[:, None] * freqs[None, :] / length
    return jnp.stack([jnp.cos(phase), -jnp.sin(phase)], axis=1).astype(jnp.bfloat16)

def whiten_level(spectra, reach):
    power = lax.optimization_barrier(jnp.sum(spectra * spectra, axis=(-3, -2)))
    bins = power.shape[-1]
    padded = jnp.pad(power, [(0, 0)] * (power.ndim - 1) + [(reach, reach)])
    total = padded[..., 0:bins]
    for offset in range(1, 2 * reach + 1):
        total = total + padded[..., offset:offset + bins]
    places = jnp.arange(bins, dtype=jnp.int32)
    widths = (jnp.minimum(places + reach, bins - 1) - jnp.maximum(places - reach, 0) + 1).astype(jnp.float32)
    return total / (widths * spectra.shape[-3])

def reference(raw, seg_mask, band):
    blocks = N_CHAN
    width = C // blocks
    columns = C // 2
    windows = SEGS * WSEG
    spectra = jnp.dot(raw.reshape(C * windows, W), transform_table(W, K), preferred_element_type=jnp.float32)
    spectra = spectra.reshape(C, SEGS, WSEG, 2, K)
    level = whiten_level(spectra, R)
    flags = seg_mask.astype(jnp.float32)
    white = spectra * flags[:, :, None, None, None] * lax.rsqrt(level + EPSILON)[:, :, None, None, :]
    white = white.astype(jnp.bfloat16).reshape(C, windows, 2, K)
    extended = jnp.concatenate([white, white[:columns]], axis=0)
    flag_ext = jnp.concatenate([flags, flags[:columns]], axis=0)
    table = lag_table(W, K, MAXLAG).astype(jnp.float32)

    def one_block(index):
        first = index * width
        start = (first - C // 4) % C
        mine = lax.dynamic_slice_in_dim(white, first, width, 0).astype(jnp.float32)
        others = lax.dynamic_slice_in_dim(extended, start, columns, 0).astype(jnp.float32)
        real_part = jnp.einsum('iwpf,jwpf->fij', mine, others)
        imag_part = jnp.einsum('iwf,jwf->fij', mine[:, :, 1], others[:, :, 0]) - jnp.einsum('iwf,jwf->fij', mine[:, :, 0], others[:, :, 1])
        row_flags = lax.dynamic_slice_in_dim(flags, first, width, 0)
        col_flags = lax.dynamic_slice_in_dim(flag_ext, start, columns, 0)
        counts = WSEG * jnp.dot(row_flags, col_flags.T, precision=lax.Precision.HIGHEST, preferred_element_type=jnp.float32)
        stack = (jnp.stack([real_part, imag_part], axis=0) / jnp.maximum(counts, 1.0)[None, None]).astype(jnp.bfloat16)
        stack = lax.optimization_barrier(stack).astype(jnp.float32)
        lagged = jnp.einsum('tpf,pfij->itj', table, stack)
        row_ids = first + jnp.arange(width, dtype=jnp.int32)
        col_ids = (first - C // 4 + jnp.arange(columns, dtype=jnp.int32)) % C
        diff = (col_ids[None, :] - row_ids[:, None]) % C
        distance = jnp.minimum(diff, C - diff)
        limits = lax.dynamic_slice_in_dim(band, first, width, 0)
        keep = (distance >= limits[:, 0:1]) & (distance <= limits[:, 1:2])
        return jnp.where(keep[:, None, :], lagged, 0.0).astype(jnp.bfloat16)
    result = lax.map(one_block, jnp.arange(blocks, dtype=jnp.int32))
    return result.reshape(C, 2 * MAXLAG + 1, columns)
```

```python
import math

import jax
import jax.numpy as jnp
from jax import lax
from jax.experimental import pallas as pl
from jax.experimental.pallas import tpu as pltpu
from jax.sharding import PartitionSpec as P

C = 1024
W = 512
K = 128
MAXLAG = 200
R = 4
WSEG = 32


EPSILON = 1e-06


def passed_along(value, axis, by):
    length = lax.axis_size(axis)
    return lax.ppermute(value, axis, [(i, (i + by) % length) for i in range(length)])


def transform_table(length, bins):
    samples = jnp.arange(length, dtype=jnp.float32)
    freqs = jnp.arange(1, bins + 1, dtype=jnp.float32)
    phase = 2.0 * math.pi * samples[:, None] * freqs[None, :] / length
    taper = 0.5 - 0.5 * jnp.cos(2.0 * math.pi * samples / length)
    weight = taper[:, None] / math.sqrt(length)
    return jnp.concatenate([weight * jnp.cos(phase), -weight * jnp.sin(phase)], axis=1).astype(
        jnp.bfloat16
    )


def lag_table(length, bins, reach):
    shifts = jnp.arange(-reach, reach + 1, dtype=jnp.float32)
    freqs = jnp.arange(1, bins + 1, dtype=jnp.float32)
    phase = 2.0 * math.pi * shifts[:, None] * freqs[None, :] / length
    return jnp.stack([jnp.cos(phase), -jnp.sin(phase)], axis=1).astype(jnp.bfloat16)


def whiten_level(spectra, reach):
    power = jnp.sum(spectra * spectra, axis=(-3, -2))
    bins = power.shape[-1]
    padded = jnp.pad(power, [(0, 0)] * (power.ndim - 1) + [(reach, reach)])
    total = padded[..., 0:bins]
    for offset in range(1, 2 * reach + 1):
        total = total + padded[..., offset : offset + bins]
    places = jnp.arange(bins, dtype=jnp.int32)
    widths = (jnp.minimum(places + reach, bins - 1) - jnp.maximum(places - reach, 0) + 1).astype(
        jnp.float32
    )
    return total / (widths * spectra.shape[-3])


def ring_body(raw, seg_mask, band):
    rows = raw.shape[0]
    seg_count = raw.shape[1] // (WSEG * W)
    windows = seg_count * WSEG
    chan_count = lax.axis_size("chan")
    seg_size = lax.axis_size("seg")
    chan_index = lax.axis_index("chan")
    seg_index = lax.axis_index("seg")
    half_blocks = chan_count // 4
    columns = C // 2
    own_width = columns // seg_size
    frames = raw.reshape(rows * windows, W)
    spectra = jnp.dot(frames, transform_table(W, K), preferred_element_type=jnp.float32)
    spectra = spectra.reshape(rows, seg_count, WSEG, 2, K)
    level = whiten_level(spectra, R)
    own_flags = lax.dynamic_slice_in_dim(seg_mask, seg_index * seg_count, seg_count, 1).astype(
        jnp.float32
    )
    white = (
        spectra
        * own_flags[:, :, None, None, None]
        * lax.rsqrt(level + EPSILON)[:, :, None, None, :]
    )
    white = white.astype(jnp.bfloat16)
    local = jnp.transpose(white, (4, 0, 3, 1, 2)).reshape(K, rows, 2 * windows)
    flag_all = seg_mask.astype(jnp.bfloat16)
    bins = local.shape[0]

    def absorb(state, remote, remote_flags, slot):
        totals, counts = state
        grouped = remote.reshape(bins, rows, -1, 2, windows)
        rotated = jnp.stack([-grouped[:, :, :, 1], grouped[:, :, :, 0]], axis=3).reshape(
            remote.shape
        )
        partner = jnp.concatenate([remote, rotated], axis=1)
        product = jnp.einsum("fil,fjl->fij", local, partner, preferred_element_type=jnp.float32)
        product = product.reshape(bins, rows, 2, rows)
        totals = lax.dynamic_update_slice_in_dim(totals, product, slot * rows, 3)
        pair_count = WSEG * jnp.dot(flag_all, remote_flags.T, preferred_element_type=jnp.float32)
        counts = lax.dynamic_update_slice_in_dim(counts, pair_count, slot * rows, 1)
        return (totals, counts)

    start_state = (
        jnp.zeros((bins, rows, 2, columns), jnp.float32),
        jnp.zeros((rows, columns), jnp.float32),
    )
    state = absorb(start_state, local, flag_all, half_blocks)

    def step_lower(pair):
        return passed_along((pair[0], pair[1]), "chan", 1)

    def both_turn(index, carry):
        state, below, above = carry
        below = step_lower(below)
        above = passed_along((above[0], above[1]), "chan", -1)
        state = absorb(state, below[0], below[1], half_blocks - 1 - index)
        state = absorb(state, above[0], above[1], half_blocks + 1 + index)
        return (state, below, above)

    state, below, above = lax.fori_loop(
        0, half_blocks - 1, both_turn, (state, (local, flag_all), (local, flag_all))
    )
    below = step_lower(below)
    state = absorb(state, below[0], below[1], 0)
    totals, counts = state
    own_totals = lax.psum_scatter(totals, "seg", scatter_dimension=3, tiled=True)
    own_counts = lax.dynamic_slice_in_dim(counts, seg_index * own_width, own_width, 1)
    stack = (own_totals / jnp.maximum(own_counts, 1.0)[None, :, None, :]).astype(jnp.bfloat16)
    lagged = jnp.einsum(
        "tpf,fipj->itj", lag_table(W, K, MAXLAG), stack, preferred_element_type=jnp.float32
    )
    row_ids = chan_index * rows + jnp.arange(rows, dtype=jnp.int32)
    col_ids = (
        chan_index * rows - C // 4 + seg_index * own_width + jnp.arange(own_width, dtype=jnp.int32)
    ) % C
    diff = (col_ids[None, :] - row_ids[:, None]) % C
    distance = jnp.minimum(diff, C - diff)
    keep = (distance >= band[:, 0:1]) & (distance <= band[:, 1:2])
    return jnp.where(keep[:, None, :], lagged, 0.0).astype(jnp.bfloat16)


def whiten_kernel(raw_ref, table_ref, flag_ref, out_ref, spec, power, padded):
    rows = raw_ref.shape[0]
    bins = table_ref.shape[0] // 2
    wseg = raw_ref.shape[1] // W
    power[...] = jnp.zeros_like(power)
    table = table_ref[...]

    def transform(pair, _):
        start = pl.multiple_of(pair * 2 * W, 2 * W)
        frames = jnp.concatenate(
            [raw_ref[:, pl.ds(start, W)], raw_ref[:, pl.ds(start + W, W)]], axis=0
        )
        both = lax.dot_general(
            table, frames, (((1,), (1,)), ((), ())), preferred_element_type=jnp.float32
        )
        for part in range(2):
            value = both[:, part * rows : (part + 1) * rows]
            window = pair * 2 + part
            real, imag = value[:bins], value[bins:]
            spec[pl.ds(pl.multiple_of(window * bins, bins), bins), :] = real
            spec[pl.ds(pl.multiple_of((wseg + window) * bins, bins), bins), :] = imag
            power[...] += real * real + imag * imag
        return 0

    lax.fori_loop(0, wseg // 2, transform, 0, unroll=2)
    padded[...] = jnp.zeros_like(padded)
    padded[pl.ds(8, bins), :] = power[...]
    total = padded[pl.ds(8 - R, bins), :]
    for offset in range(1, 2 * R + 1):
        total = total + padded[pl.ds(8 - R + offset, bins), :]
    places = lax.broadcasted_iota(jnp.int32, (bins, rows), 0)
    widths = jnp.minimum(places + R, bins - 1) - jnp.maximum(places - R, 0) + 1
    level = total / (widths.astype(jnp.float32) * wseg)
    power[...] = flag_ref[0] * lax.rsqrt(level + EPSILON)

    def place(f, _):
        tile = spec[pl.ds(f, 2 * wseg, stride=bins), :]
        out_ref[f] = (tile * power[pl.ds(f, 1), :]).astype(jnp.bfloat16)
        return 0

    lax.fori_loop(0, bins, place, 0, unroll=8)


def whiten(raw, flags):
    rows = raw.shape[0]
    seg_count = raw.shape[1] // (WSEG * W)
    return pl.pallas_call(
        whiten_kernel,
        grid=(seg_count,),
        in_specs=[
            pl.BlockSpec((rows, WSEG * W), lambda s: (0, s)),
            pl.BlockSpec((2 * K, W), lambda s: (0, 0)),
            pl.BlockSpec((1, 1, rows), lambda s: (s, 0, 0)),
        ],
        out_specs=pl.BlockSpec((K, 2 * WSEG, rows), lambda s: (0, s, 0)),
        out_shape=jax.ShapeDtypeStruct((K, seg_count * 2 * WSEG, rows), jnp.bfloat16),
        scratch_shapes=[
            pltpu.VMEM((2 * WSEG * K, rows), jnp.float32),
            pltpu.VMEM((K, rows), jnp.float32),
            pltpu.VMEM((K + 16, rows), jnp.float32),
        ],
        compiler_params=pltpu.CompilerParams(vmem_limit_bytes=40 * 2**20),
        cost_estimate=pl.CostEstimate(
            flops=4 * raw.size * K, bytes_accessed=raw.size * 4, transcendentals=0
        ),
        name="whiten",
    )(raw, transform_table(W, K).T, flags.T[:, None, :])


FBLOCK = 16
IBLOCK = 8


def pair_kernel(f_steps, own1, own2, far1, far2, recip, keep, table, *rest):
    out_ref, cross = rest[-2:]
    step = pl.program_id(0)
    rows = own1.shape[2]
    bins = cross.shape[0] // (2 * rows)
    lags = out_ref.shape[1]

    @pl.when(step < f_steps)
    def _():
        for g in range(FBLOCK):
            own = jnp.concatenate([own1[g], own2[g]], axis=0)
            turned = []
            for seg in range(own.shape[0] // (2 * WSEG)):
                first = seg * 2 * WSEG
                turned.append(own[first + WSEG : first + 2 * WSEG])
                turned.append(-own[first : first + WSEG])
            left = jnp.concatenate([own, jnp.concatenate(turned, axis=0)], axis=1)
            right = jnp.concatenate([far1[g], far2[g]], axis=0)
            value = lax.dot_general(
                left, right, (((0,), (0,)), ((), ())), preferred_element_type=jnp.float32
            )
            start = pl.multiple_of((step * FBLOCK + g) * 2 * rows, 2 * rows)
            cross[pl.ds(start, 2 * rows), :] = value

    @pl.when(step >= f_steps)
    def _():
        lag = table[...]
        for pair in range(IBLOCK // 2):
            sides = []
            for part in range(2):
                i = (step - f_steps) * IBLOCK + pair * 2 + part
                scale = recip[pl.ds(i, 1), :]
                halves = [
                    (cross[pl.ds(p * rows + i, bins, stride=2 * rows), :] * scale).astype(
                        jnp.bfloat16
                    )
                    for p in range(2)
                ]
                sides.append(jnp.concatenate(halves, axis=0))
            lagged = jnp.dot(
                lag, jnp.concatenate(sides, axis=1), preferred_element_type=jnp.float32
            )
            for part in range(2):
                i = (step - f_steps) * IBLOCK + pair * 2 + part
                inside = keep[pl.ds(i, 1), :] > 0.0
                value = lagged[:lags, part * rows : (part + 1) * rows]
                out_ref[pair * 2 + part] = jnp.where(inside, value, 0.0).astype(jnp.bfloat16)


def pair_block(own1, own2, far1, far2, recip, keep, table, place, halves, previous=None):
    bins, depth, rows = own1.shape
    f_steps = bins // FBLOCK
    i_steps = rows // IBLOCK
    lags = 2 * MAXLAG + 1
    white = pl.BlockSpec((FBLOCK, depth, rows), lambda g: (jnp.minimum(g, f_steps - 1), 0, 0))
    square = pl.BlockSpec((rows, rows), lambda g: (0, 0))
    specs = [white] * 4 + [square] * 2 + [pl.BlockSpec(table.shape, lambda g: (0, 0))]
    args = [own1, own2, far1, far2, recip, keep, table]
    aliases = {}
    if previous is not None:
        aliases = {len(args): 0}
        specs.append(pl.BlockSpec(memory_space=pl.ANY))
        args.append(previous)
    return pl.pallas_call(
        lambda *refs: pair_kernel(f_steps, *refs),
        grid=(f_steps + i_steps,),
        in_specs=specs,
        out_specs=pl.BlockSpec(
            (IBLOCK, lags, rows), lambda g: (jnp.maximum(g - f_steps, 0), 0, place)
        ),
        out_shape=jax.ShapeDtypeStruct((rows, lags, halves * rows), jnp.bfloat16),
        scratch_shapes=[pltpu.VMEM((bins * 2 * rows, rows), jnp.float32)],
        input_output_aliases=aliases,
        compiler_params=pltpu.CompilerParams(vmem_limit_bytes=44 * 2**20),
        cost_estimate=pl.CostEstimate(
            flops=8 * bins * rows * rows * (2 * depth + lags) // 2,
            bytes_accessed=bins * depth * rows * 8 + rows * rows * lags * 2,
            transcendentals=0,
        ),
        name="pair_block_%d" % place,
    )(*args)


def direct_body(raw, seg_mask, band):
    rows = raw.shape[0]
    seg_count = raw.shape[1] // (WSEG * W)
    n = lax.axis_size("chan")
    chan_index = lax.axis_index("chan")
    seg_index = lax.axis_index("seg")
    flags = seg_mask.astype(jnp.float32)
    own_flags = lax.dynamic_slice_in_dim(flags, seg_index * seg_count, seg_count, 1)

    def send(value, pairs):
        return lax.ppermute(
            value, ("chan", "seg"), [(a % n * 2 + s, b % n * 2 + t) for a, s, b, t in pairs]
        )

    blocks = range(n)
    y_first = [(b, 0, b + 2, 0) for b in blocks] + [(b, 1, b, 1) for b in blocks]
    y_second = [(b, 1, b + 2, 0) for b in blocks] + [(b, 0, b, 1) for b in blocks]
    x_first = [(b, 0, b + 1, 0) for b in blocks] + [(b, 1, b - 1, 1) for b in blocks]
    x_second = [(b, 1, b + 1, 0) for b in blocks] + [(b, 0, b - 1, 1) for b in blocks]
    y_flags = send(flags, y_first)
    x_flags = send(flags, x_first)
    white = whiten(raw, own_flags)
    own_other = send(white, [(b, s, b, 1 - s) for b in blocks for s in range(2)])

    y1 = send(white, y_first)
    y2 = send(white, y_second)
    x1 = send(white, x_first)
    x2 = send(white, x_second)

    table = lag_table(W, K, MAXLAG).reshape(2 * MAXLAG + 1, 2 * K)
    table = jnp.pad(table, ((0, -table.shape[0] % 16), (0, 0)))
    row_ids = chan_index * rows + jnp.arange(rows, dtype=jnp.int32)

    def factors(far_flags, block):
        counts = WSEG * jnp.sum(flags[:, None, :] * far_flags[None, :, :], axis=-1)
        col_ids = (block * rows + jnp.arange(rows, dtype=jnp.int32)) % C
        diff = (col_ids[None, :] - row_ids[:, None]) % C
        distance = jnp.minimum(diff, C - diff)
        keep = (distance >= band[:, 0:1]) & (distance <= band[:, 1:2])
        return 1.0 / jnp.maximum(counts, 1.0), keep.astype(jnp.float32)

    y_recip, y_keep = factors(y_flags, chan_index - 2 + 2 * seg_index)
    x_recip, x_keep = factors(x_flags, chan_index - 1 + 2 * seg_index)
    out = pair_block(white, own_other, y1, y2, y_recip, y_keep, table, 0, 2)
    return pair_block(white, own_other, x1, x2, x_recip, x_keep, table, 1, 2, out)


def solution(mesh):
    in_specs = (P(("sub", "chan"), "seg"), P(("sub", "chan"), None), P(("sub", "chan"), None))
    out_specs = P(("sub", "chan"), None, "seg")
    direct = mesh.shape["chan"] == 8 and mesh.shape["seg"] == 2
    body = direct_body if direct else ring_body
    return jax.shard_map(body, mesh=mesh, in_specs=in_specs, out_specs=out_specs, check_vma=False)
```

```python
import math

import jax
import jax.numpy as jnp
from jax import lax
from jax.experimental import pallas as pl
from jax.experimental.pallas import tpu as pltpu
from jax.sharding import PartitionSpec as P

C = 1024
W = 512
K = 128
MAXLAG = 200
R = 4
WSEG = 32


EPSILON = 1e-06


def passed_along(value, axis, by):
    length = lax.axis_size(axis)
    return lax.ppermute(value, axis, [(i, (i + by) % length) for i in range(length)])


def transform_table(length, bins):
    samples = jnp.arange(length, dtype=jnp.float32)
    freqs = jnp.arange(1, bins + 1, dtype=jnp.float32)
    phase = 2.0 * math.pi * samples[:, None] * freqs[None, :] / length
    taper = 0.5 - 0.5 * jnp.cos(2.0 * math.pi * samples / length)
    weight = taper[:, None] / math.sqrt(length)
    return jnp.concatenate([weight * jnp.cos(phase), -weight * jnp.sin(phase)], axis=1).astype(
        jnp.bfloat16
    )


def lag_table(length, bins, reach):
    shifts = jnp.arange(-reach, reach + 1, dtype=jnp.float32)
    freqs = jnp.arange(1, bins + 1, dtype=jnp.float32)
    phase = 2.0 * math.pi * shifts[:, None] * freqs[None, :] / length
    return jnp.stack([jnp.cos(phase), -jnp.sin(phase)], axis=1).astype(jnp.bfloat16)


def whiten_level(spectra, reach):
    power = jnp.sum(spectra * spectra, axis=(-3, -2))
    bins = power.shape[-1]
    padded = jnp.pad(power, [(0, 0)] * (power.ndim - 1) + [(reach, reach)])
    total = padded[..., 0:bins]
    for offset in range(1, 2 * reach + 1):
        total = total + padded[..., offset : offset + bins]
    places = jnp.arange(bins, dtype=jnp.int32)
    widths = (jnp.minimum(places + reach, bins - 1) - jnp.maximum(places - reach, 0) + 1).astype(
        jnp.float32
    )
    return total / (widths * spectra.shape[-3])


def ring_body(raw, seg_mask, band):
    rows = raw.shape[0]
    seg_count = raw.shape[1] // (WSEG * W)
    windows = seg_count * WSEG
    chan_count = lax.axis_size("chan")
    seg_size = lax.axis_size("seg")
    chan_index = lax.axis_index("chan")
    seg_index = lax.axis_index("seg")
    half_blocks = chan_count // 4
    columns = C // 2
    own_width = columns // seg_size
    frames = raw.reshape(rows * windows, W)
    spectra = jnp.dot(frames, transform_table(W, K), preferred_element_type=jnp.float32)
    spectra = spectra.reshape(rows, seg_count, WSEG, 2, K)
    level = whiten_level(spectra, R)
    own_flags = lax.dynamic_slice_in_dim(seg_mask, seg_index * seg_count, seg_count, 1).astype(
        jnp.float32
    )
    white = (
        spectra
        * own_flags[:, :, None, None, None]
        * lax.rsqrt(level + EPSILON)[:, :, None, None, :]
    )
    white = white.astype(jnp.bfloat16)
    local = jnp.transpose(white, (4, 0, 3, 1, 2)).reshape(K, rows, 2 * windows)
    flag_all = seg_mask.astype(jnp.bfloat16)
    bins = local.shape[0]

    def absorb(state, remote, remote_flags, slot):
        totals, counts = state
        grouped = remote.reshape(bins, rows, -1, 2, windows)
        rotated = jnp.stack([-grouped[:, :, :, 1], grouped[:, :, :, 0]], axis=3).reshape(
            remote.shape
        )
        partner = jnp.concatenate([remote, rotated], axis=1)
        product = jnp.einsum("fil,fjl->fij", local, partner, preferred_element_type=jnp.float32)
        product = product.reshape(bins, rows, 2, rows)
        totals = lax.dynamic_update_slice_in_dim(totals, product, slot * rows, 3)
        pair_count = WSEG * jnp.dot(flag_all, remote_flags.T, preferred_element_type=jnp.float32)
        counts = lax.dynamic_update_slice_in_dim(counts, pair_count, slot * rows, 1)
        return (totals, counts)

    start_state = (
        jnp.zeros((bins, rows, 2, columns), jnp.float32),
        jnp.zeros((rows, columns), jnp.float32),
    )
    state = absorb(start_state, local, flag_all, half_blocks)

    def step_lower(pair):
        return passed_along((pair[0], pair[1]), "chan", 1)

    def both_turn(index, carry):
        state, below, above = carry
        below = step_lower(below)
        above = passed_along((above[0], above[1]), "chan", -1)
        state = absorb(state, below[0], below[1], half_blocks - 1 - index)
        state = absorb(state, above[0], above[1], half_blocks + 1 + index)
        return (state, below, above)

    state, below, above = lax.fori_loop(
        0, half_blocks - 1, both_turn, (state, (local, flag_all), (local, flag_all))
    )
    below = step_lower(below)
    state = absorb(state, below[0], below[1], 0)
    totals, counts = state
    own_totals = lax.psum_scatter(totals, "seg", scatter_dimension=3, tiled=True)
    own_counts = lax.dynamic_slice_in_dim(counts, seg_index * own_width, own_width, 1)
    stack = (own_totals / jnp.maximum(own_counts, 1.0)[None, :, None, :]).astype(jnp.bfloat16)
    lagged = jnp.einsum(
        "tpf,fipj->itj", lag_table(W, K, MAXLAG), stack, preferred_element_type=jnp.float32
    )
    row_ids = chan_index * rows + jnp.arange(rows, dtype=jnp.int32)
    col_ids = (
        chan_index * rows - C // 4 + seg_index * own_width + jnp.arange(own_width, dtype=jnp.int32)
    ) % C
    diff = (col_ids[None, :] - row_ids[:, None]) % C
    distance = jnp.minimum(diff, C - diff)
    keep = (distance >= band[:, 0:1]) & (distance <= band[:, 1:2])
    return jnp.where(keep[:, None, :], lagged, 0.0).astype(jnp.bfloat16)


def whiten_kernel(raw_ref, table_ref, flag_ref, out_ref, spec, power, padded):
    rows = raw_ref.shape[0]
    bins = table_ref.shape[0] // 2
    wseg = raw_ref.shape[1] // W
    power[...] = jnp.zeros_like(power)
    table = table_ref[...]

    def transform(pair, _):
        start = pl.multiple_of(pair * 2 * W, 2 * W)
        frames = jnp.concatenate(
            [raw_ref[:, pl.ds(start, W)], raw_ref[:, pl.ds(start + W, W)]], axis=0
        )
        both = lax.dot_general(
            table, frames, (((1,), (1,)), ((), ())), preferred_element_type=jnp.float32
        )
        for part in range(2):
            value = both[:, part * rows : (part + 1) * rows]
            window = pair * 2 + part
            real, imag = value[:bins], value[bins:]
            spec[pl.ds(pl.multiple_of(window * bins, bins), bins), :] = real
            spec[pl.ds(pl.multiple_of((wseg + window) * bins, bins), bins), :] = imag
            power[...] += real * real + imag * imag
        return 0

    lax.fori_loop(0, wseg // 2, transform, 0, unroll=4)
    padded[...] = jnp.zeros_like(padded)
    padded[pl.ds(8, bins), :] = power[...]
    total = padded[pl.ds(8 - R, bins), :]
    for offset in range(1, 2 * R + 1):
        total = total + padded[pl.ds(8 - R + offset, bins), :]
    places = lax.broadcasted_iota(jnp.int32, (bins, rows), 0)
    widths = jnp.minimum(places + R, bins - 1) - jnp.maximum(places - R, 0) + 1
    level = total / (widths.astype(jnp.float32) * wseg)
    power[...] = flag_ref[0] * lax.rsqrt(level + EPSILON)

    def place(f, _):
        tile = spec[pl.ds(f, 2 * wseg, stride=bins), :]
        out_ref[f] = (tile * power[pl.ds(f, 1), :]).astype(jnp.bfloat16)
        return 0

    lax.fori_loop(0, bins, place, 0, unroll=8)


def whiten(raw, flags):
    rows = raw.shape[0]
    seg_count = raw.shape[1] // (WSEG * W)
    return pl.pallas_call(
        whiten_kernel,
        grid=(seg_count,),
        in_specs=[
            pl.BlockSpec((rows, WSEG * W), lambda s: (0, s)),
            pl.BlockSpec((2 * K, W), lambda s: (0, 0)),
            pl.BlockSpec((1, 1, rows), lambda s: (s, 0, 0)),
        ],
        out_specs=pl.BlockSpec((K, 2 * WSEG, rows), lambda s: (0, s, 0)),
        out_shape=jax.ShapeDtypeStruct((K, seg_count * 2 * WSEG, rows), jnp.bfloat16),
        scratch_shapes=[
            pltpu.VMEM((2 * WSEG * K, rows), jnp.float32),
            pltpu.VMEM((K, rows), jnp.float32),
            pltpu.VMEM((K + 16, rows), jnp.float32),
        ],
        compiler_params=pltpu.CompilerParams(vmem_limit_bytes=56 * 2**20),
        cost_estimate=pl.CostEstimate(
            flops=4 * raw.size * K, bytes_accessed=raw.size * 4, transcendentals=0
        ),
        name="whiten",
    )(raw, transform_table(W, K).T, flags.T[:, None, :])


FBLOCK = 16
IBLOCK = 16


def pair_kernel(f_steps, n_far, own1, own2, *refs):
    fars, (recip, keep, table), rest = refs[:n_far], refs[n_far : n_far + 3], refs[n_far + 3 :]
    out_ref, cross, turning = rest[-3:]
    step = pl.program_id(0)
    rows = own1.shape[2]
    bins = cross.shape[0] // (2 * rows)
    lags = out_ref.shape[0]

    @pl.when(step < f_steps)
    def _():
        for g in range(FBLOCK):
            own = jnp.concatenate([own1[g], own2[g]], axis=0)
            turned = []
            for seg in range(own.shape[0] // (2 * WSEG)):
                first = seg * 2 * WSEG
                turned.append(own[first + WSEG : first + 2 * WSEG])
                turned.append(-own[first : first + WSEG])
            left = jnp.concatenate([own, jnp.concatenate(turned, axis=0)], axis=1)
            if n_far == 2:
                right = jnp.concatenate([far[g] for far in fars], axis=0)
            else:
                right = jnp.concatenate(
                    [fars[0][g] + fars[2][g], fars[1][g] + fars[3][g]], axis=0
                )
            value = lax.dot_general(
                left, right, (((0,), (0,)), ((), ())), preferred_element_type=jnp.float32
            )
            start = pl.multiple_of((step * FBLOCK + g) * 2 * rows, 2 * rows)
            cross[pl.ds(start, 2 * rows), :] = value

    @pl.when(step >= f_steps)
    def _():
        lag = table[...]
        for pair in range(IBLOCK // 2):
            sides = []
            for part in range(2):
                i = (step - f_steps) * IBLOCK + pair * 2 + part
                scale = recip[pl.ds(i, 1), :]
                halves = [
                    (cross[pl.ds(p * rows + i, bins, stride=2 * rows), :] * scale).astype(
                        jnp.bfloat16
                    )
                    for p in range(2)
                ]
                sides.append(jnp.concatenate(halves, axis=0))
            lagged = jnp.dot(
                lag, jnp.concatenate(sides, axis=1), preferred_element_type=jnp.float32
            )
            for part in range(2):
                i = (step - f_steps) * IBLOCK + pair * 2 + part
                inside = keep[pl.ds(i, 1), :] > 0.0
                value = lagged[:lags, part * rows : (part + 1) * rows]
                turning[pl.ds(pair * 2 + part, lags, stride=IBLOCK), :] = jnp.where(
                    inside, value, 0.0
                )
        out_ref[...] = turning[...].reshape(lags, IBLOCK, rows).astype(jnp.bfloat16)


def pair_block(own1, own2, fars, recip, keep, table, place, halves, previous=None):
    bins, depth, rows = own1.shape
    f_steps = bins // FBLOCK
    i_steps = rows // IBLOCK
    lags = 2 * MAXLAG + 1
    white = pl.BlockSpec((FBLOCK, depth, rows), lambda g: (jnp.minimum(g, f_steps - 1), 0, 0))
    square = pl.BlockSpec((rows, rows), lambda g: (0, 0))
    specs = [white] * (2 + len(fars)) + [square] * 2 + [pl.BlockSpec(table.shape, lambda g: (0, 0))]
    args = [own1, own2, *fars, recip, keep, table]
    aliases = {}
    if previous is not None:
        aliases = {len(args): 0}
        specs.append(pl.BlockSpec(memory_space=pl.ANY))
        args.append(previous)
    return pl.pallas_call(
        lambda *refs: pair_kernel(f_steps, len(fars), *refs),
        grid=(f_steps + i_steps,),
        in_specs=specs,
        out_specs=pl.BlockSpec(
            (lags, IBLOCK, rows), lambda g: (0, jnp.maximum(g - f_steps, 0), place)
        ),
        out_shape=jax.ShapeDtypeStruct((lags, rows, halves * rows), jnp.bfloat16),
        scratch_shapes=[
            pltpu.VMEM((bins * 2 * rows, rows), jnp.float32),
            pltpu.VMEM((lags * IBLOCK, rows), jnp.float32),
        ],
        input_output_aliases=aliases,
        compiler_params=pltpu.CompilerParams(vmem_limit_bytes=44 * 2**20),
        cost_estimate=pl.CostEstimate(
            flops=8 * bins * rows * rows * (2 * depth + lags) // 2,
            bytes_accessed=bins * depth * rows * 8 + rows * rows * lags * 2,
            transcendentals=0,
        ),
        name="pair_block_%d" % place,
    )(*args)


def direct_body(raw, seg_mask, band):
    rows = raw.shape[0]
    seg_count = raw.shape[1] // (WSEG * W)
    n = lax.axis_size("chan")
    chan_index = lax.axis_index("chan")
    seg_index = lax.axis_index("seg")
    flags = seg_mask.astype(jnp.float32)
    own_flags = lax.dynamic_slice_in_dim(flags, seg_index * seg_count, seg_count, 1)

    def send(value, pairs):
        return lax.ppermute(
            value, ("chan", "seg"), [(a % n * 2 + s, b % n * 2 + t) for a, s, b, t in pairs]
        )

    blocks = range(n)
    near = [b for b in blocks if b % 2 == 0]
    odd = [b for b in blocks if b % 2 == 1]
    y_first = [(b, 0, b + 2, 0) for b in blocks] + [(b, 1, b, 1) for b in blocks]
    y_second = [(b, 1, b + 2, 0) for b in blocks] + [(b, 0, b, 1) for b in blocks]
    x_pairs = [
        [(b, s, b + 1, 0) for b in ups] + [(b, 1 - s, b - 1, 1) for b in downs]
        for ups, downs in ((near, odd), (odd, near))
        for s in range(2)
    ]
    x_flag_pairs = [(b, 0, b + 1, 0) for b in blocks] + [(b, 1, b - 1, 1) for b in blocks]
    white, late_flags = lax.optimization_barrier((whiten(raw, own_flags), flags))
    y_flags = send(late_flags, y_first)
    x_flags = send(late_flags, x_flag_pairs)
    own_other = send(white, [(b, s, b, 1 - s) for b in blocks for s in range(2)])
    y1 = send(white, y_first)
    y2 = send(white, y_second)
    x1 = send(white, x_pairs[0])
    x2 = send(white, x_pairs[1])
    white, own_other, y1, y2, x1, x2, y_flags, x_flags = lax.optimization_barrier(
        (white, own_other, y1, y2, x1, x2, y_flags, x_flags)
    )
    x3 = send(white, x_pairs[2])
    x4 = send(white, x_pairs[3])

    table = lag_table(W, K, MAXLAG).reshape(2 * MAXLAG + 1, 2 * K)
    table = jnp.pad(table, ((0, -table.shape[0] % 16), (0, 0)))
    row_ids = chan_index * rows + jnp.arange(rows, dtype=jnp.int32)

    def factors(far_flags, block):
        counts = WSEG * jnp.sum(flags[:, None, :] * far_flags[None, :, :], axis=-1)
        col_ids = (block * rows + jnp.arange(rows, dtype=jnp.int32)) % C
        diff = (col_ids[None, :] - row_ids[:, None]) % C
        distance = jnp.minimum(diff, C - diff)
        keep = (distance >= band[:, 0:1]) & (distance <= band[:, 1:2])
        return 1.0 / jnp.maximum(counts, 1.0), keep.astype(jnp.float32)

    y_recip, y_keep = factors(y_flags, chan_index - 2 + 2 * seg_index)
    x_recip, x_keep = factors(x_flags, chan_index - 1 + 2 * seg_index)
    out = pair_block(white, own_other, (y1, y2), y_recip, y_keep, table, 0, 2)
    out = pair_block(white, own_other, (x1, x2, x3, x4), x_recip, x_keep, table, 1, 2, out)
    return jnp.transpose(out, (1, 0, 2))


def solution(mesh):
    in_specs = (P(("sub", "chan"), "seg"), P(("sub", "chan"), None), P(("sub", "chan"), None))
    out_specs = P(("sub", "chan"), None, "seg")
    direct = mesh.shape["chan"] == 8 and mesh.shape["seg"] == 2
    body = direct_body if direct else ring_body
    return jax.shard_map(body, mesh=mesh, in_specs=in_specs, out_specs=out_specs, check_vma=False)
```

```python
import math

import jax
import jax.numpy as jnp
from jax import lax
from jax.experimental import pallas as pl
from jax.experimental.pallas import tpu as pltpu
from jax.sharding import PartitionSpec as P

C = 1024
W = 512
K = 128
MAXLAG = 200
R = 4
WSEG = 32


EPSILON = 1e-06


def passed_along(value, axis, by):
    length = lax.axis_size(axis)
    return lax.ppermute(value, axis, [(i, (i + by) % length) for i in range(length)])


def transform_table(length, bins):
    samples = jnp.arange(length, dtype=jnp.float32)
    freqs = jnp.arange(1, bins + 1, dtype=jnp.float32)
    phase = 2.0 * math.pi * samples[:, None] * freqs[None, :] / length
    taper = 0.5 - 0.5 * jnp.cos(2.0 * math.pi * samples / length)
    weight = taper[:, None] / math.sqrt(length)
    return jnp.concatenate([weight * jnp.cos(phase), -weight * jnp.sin(phase)], axis=1).astype(
        jnp.bfloat16
    )


def lag_table(length, bins, reach):
    shifts = jnp.arange(-reach, reach + 1, dtype=jnp.float32)
    freqs = jnp.arange(1, bins + 1, dtype=jnp.float32)
    phase = 2.0 * math.pi * shifts[:, None] * freqs[None, :] / length
    return jnp.stack([jnp.cos(phase), -jnp.sin(phase)], axis=1).astype(jnp.bfloat16)


def whiten_level(spectra, reach):
    power = jnp.sum(spectra * spectra, axis=(-3, -2))
    bins = power.shape[-1]
    padded = jnp.pad(power, [(0, 0)] * (power.ndim - 1) + [(reach, reach)])
    total = padded[..., 0:bins]
    for offset in range(1, 2 * reach + 1):
        total = total + padded[..., offset : offset + bins]
    places = jnp.arange(bins, dtype=jnp.int32)
    widths = (jnp.minimum(places + reach, bins - 1) - jnp.maximum(places - reach, 0) + 1).astype(
        jnp.float32
    )
    return total / (widths * spectra.shape[-3])


def ring_body(raw, seg_mask, band):
    rows = raw.shape[0]
    seg_count = raw.shape[1] // (WSEG * W)
    windows = seg_count * WSEG
    chan_count = lax.axis_size("chan")
    seg_size = lax.axis_size("seg")
    chan_index = lax.axis_index("chan")
    seg_index = lax.axis_index("seg")
    half_blocks = chan_count // 4
    columns = C // 2
    own_width = columns // seg_size
    frames = raw.reshape(rows * windows, W)
    spectra = jnp.dot(frames, transform_table(W, K), preferred_element_type=jnp.float32)
    spectra = spectra.reshape(rows, seg_count, WSEG, 2, K)
    level = whiten_level(spectra, R)
    own_flags = lax.dynamic_slice_in_dim(seg_mask, seg_index * seg_count, seg_count, 1).astype(
        jnp.float32
    )
    white = (
        spectra
        * own_flags[:, :, None, None, None]
        * lax.rsqrt(level + EPSILON)[:, :, None, None, :]
    )
    white = white.astype(jnp.bfloat16)
    local = jnp.transpose(white, (4, 0, 3, 1, 2)).reshape(K, rows, 2 * windows)
    flag_all = seg_mask.astype(jnp.bfloat16)
    bins = local.shape[0]

    def absorb(state, remote, remote_flags, slot):
        totals, counts = state
        grouped = remote.reshape(bins, rows, -1, 2, windows)
        rotated = jnp.stack([-grouped[:, :, :, 1], grouped[:, :, :, 0]], axis=3).reshape(
            remote.shape
        )
        partner = jnp.concatenate([remote, rotated], axis=1)
        product = jnp.einsum("fil,fjl->fij", local, partner, preferred_element_type=jnp.float32)
        product = product.reshape(bins, rows, 2, rows)
        totals = lax.dynamic_update_slice_in_dim(totals, product, slot * rows, 3)
        pair_count = WSEG * jnp.dot(flag_all, remote_flags.T, preferred_element_type=jnp.float32)
        counts = lax.dynamic_update_slice_in_dim(counts, pair_count, slot * rows, 1)
        return (totals, counts)

    start_state = (
        jnp.zeros((bins, rows, 2, columns), jnp.float32),
        jnp.zeros((rows, columns), jnp.float32),
    )
    state = absorb(start_state, local, flag_all, half_blocks)

    def step_lower(pair):
        return passed_along((pair[0], pair[1]), "chan", 1)

    def both_turn(index, carry):
        state, below, above = carry
        below = step_lower(below)
        above = passed_along((above[0], above[1]), "chan", -1)
        state = absorb(state, below[0], below[1], half_blocks - 1 - index)
        state = absorb(state, above[0], above[1], half_blocks + 1 + index)
        return (state, below, above)

    state, below, above = lax.fori_loop(
        0, half_blocks - 1, both_turn, (state, (local, flag_all), (local, flag_all))
    )
    below = step_lower(below)
    state = absorb(state, below[0], below[1], 0)
    totals, counts = state
    own_totals = lax.psum_scatter(totals, "seg", scatter_dimension=3, tiled=True)
    own_counts = lax.dynamic_slice_in_dim(counts, seg_index * own_width, own_width, 1)
    stack = (own_totals / jnp.maximum(own_counts, 1.0)[None, :, None, :]).astype(jnp.bfloat16)
    lagged = jnp.einsum(
        "tpf,fipj->itj", lag_table(W, K, MAXLAG), stack, preferred_element_type=jnp.float32
    )
    row_ids = chan_index * rows + jnp.arange(rows, dtype=jnp.int32)
    col_ids = (
        chan_index * rows - C // 4 + seg_index * own_width + jnp.arange(own_width, dtype=jnp.int32)
    ) % C
    diff = (col_ids[None, :] - row_ids[:, None]) % C
    distance = jnp.minimum(diff, C - diff)
    keep = (distance >= band[:, 0:1]) & (distance <= band[:, 1:2])
    return jnp.where(keep[:, None, :], lagged, 0.0).astype(jnp.bfloat16)


def whiten_kernel(raw_ref, table_ref, flag_ref, out_ref, spec, power, padded):
    rows = raw_ref.shape[0]
    bins = table_ref.shape[0] // 2
    wseg = raw_ref.shape[1] // W
    power[...] = jnp.zeros_like(power)
    table = table_ref[...]

    def transform(pair, _):
        start = pl.multiple_of(pair * 2 * W, 2 * W)
        frames = jnp.concatenate(
            [raw_ref[:, pl.ds(start, W)], raw_ref[:, pl.ds(start + W, W)]], axis=0
        )
        both = lax.dot_general(
            table, frames, (((1,), (1,)), ((), ())), preferred_element_type=jnp.float32
        )
        for part in range(2):
            value = both[:, part * rows : (part + 1) * rows]
            window = pair * 2 + part
            real, imag = value[:bins], value[bins:]
            spec[pl.ds(pl.multiple_of(window * bins, bins), bins), :] = real
            spec[pl.ds(pl.multiple_of((wseg + window) * bins, bins), bins), :] = imag
            power[...] += real * real + imag * imag
        return 0

    lax.fori_loop(0, wseg // 2, transform, 0, unroll=4)
    padded[...] = jnp.zeros_like(padded)
    padded[pl.ds(8, bins), :] = power[...]
    total = padded[pl.ds(8 - R, bins), :]
    for offset in range(1, 2 * R + 1):
        total = total + padded[pl.ds(8 - R + offset, bins), :]
    places = lax.broadcasted_iota(jnp.int32, (bins, rows), 0)
    widths = jnp.minimum(places + R, bins - 1) - jnp.maximum(places - R, 0) + 1
    level = total / (widths.astype(jnp.float32) * wseg)
    power[...] = flag_ref[0] * lax.rsqrt(level + EPSILON)

    def place(f, _):
        tile = spec[pl.ds(f, 2 * wseg, stride=bins), :]
        out_ref[f] = (tile * power[pl.ds(f, 1), :]).astype(jnp.bfloat16)
        return 0

    lax.fori_loop(0, bins, place, 0, unroll=8)


def whiten(raw, flags):
    rows = raw.shape[0]
    seg_count = raw.shape[1] // (WSEG * W)
    return pl.pallas_call(
        whiten_kernel,
        grid=(seg_count,),
        in_specs=[
            pl.BlockSpec((rows, WSEG * W), lambda s: (0, s)),
            pl.BlockSpec((2 * K, W), lambda s: (0, 0)),
            pl.BlockSpec((1, 1, rows), lambda s: (s, 0, 0)),
        ],
        out_specs=pl.BlockSpec((K, 2 * WSEG, rows), lambda s: (0, s, 0)),
        out_shape=jax.ShapeDtypeStruct((K, seg_count * 2 * WSEG, rows), jnp.bfloat16),
        scratch_shapes=[
            pltpu.VMEM((2 * WSEG * K, rows), jnp.float32),
            pltpu.VMEM((K, rows), jnp.float32),
            pltpu.VMEM((K + 16, rows), jnp.float32),
        ],
        compiler_params=pltpu.CompilerParams(vmem_limit_bytes=56 * 2**20),
        cost_estimate=pl.CostEstimate(
            flops=4 * raw.size * K, bytes_accessed=raw.size * 4, transcendentals=0
        ),
        name="whiten",
    )(raw, transform_table(W, K).T, flags.T[:, None, :])


FBLOCK = 16
IBLOCK = 16


def pair_kernel(f_steps, n_far, own1, own2, *refs):
    fars, (recip, keep, table), rest = refs[:n_far], refs[n_far : n_far + 3], refs[n_far + 3 :]
    out_ref, cross, turning = rest[-3:]
    step = pl.program_id(0)
    rows = own1.shape[2]
    bins = cross.shape[0] // (2 * rows)
    lags = out_ref.shape[0]

    @pl.when(step < f_steps)
    def _():
        for g in range(FBLOCK):
            own = jnp.concatenate([own1[g], own2[g]], axis=0)
            turned = []
            for seg in range(own.shape[0] // (2 * WSEG)):
                first = seg * 2 * WSEG
                turned.append(own[first + WSEG : first + 2 * WSEG])
                turned.append(-own[first : first + WSEG])
            left = jnp.concatenate([own, jnp.concatenate(turned, axis=0)], axis=1)
            if n_far == 2:
                right = jnp.concatenate([far[g] for far in fars], axis=0)
            else:
                right = jnp.concatenate(
                    [fars[0][g] + fars[2][g], fars[1][g] + fars[3][g]], axis=0
                )
            value = lax.dot_general(
                left, right, (((0,), (0,)), ((), ())), preferred_element_type=jnp.float32
            )
            start = pl.multiple_of((step * FBLOCK + g) * 2 * rows, 2 * rows)
            cross[pl.ds(start, 2 * rows), :] = value

    @pl.when(step >= f_steps)
    def _():
        lag = table[...]
        for pair in range(IBLOCK // 2):
            sides = []
            for part in range(2):
                i = (step - f_steps) * IBLOCK + pair * 2 + part
                scale = recip[pl.ds(i, 1), :]
                halves = [
                    (cross[pl.ds(p * rows + i, bins, stride=2 * rows), :] * scale).astype(
                        jnp.bfloat16
                    )
                    for p in range(2)
                ]
                sides.append(jnp.concatenate(halves, axis=0))
            lagged = jnp.dot(
                lag, jnp.concatenate(sides, axis=1), preferred_element_type=jnp.float32
            )
            for part in range(2):
                i = (step - f_steps) * IBLOCK + pair * 2 + part
                inside = keep[pl.ds(i, 1), :] > 0.0
                value = lagged[:lags, part * rows : (part + 1) * rows]
                turning[pl.ds(pair * 2 + part, lags, stride=IBLOCK), :] = jnp.where(
                    inside, value, 0.0
                )
        out_ref[...] = turning[...].reshape(lags, IBLOCK, rows).astype(jnp.bfloat16)


def pair_block(own1, own2, fars, recip, keep, table, place, halves, previous=None):
    bins, depth, rows = own1.shape
    f_steps = bins // FBLOCK
    i_steps = rows // IBLOCK
    lags = 2 * MAXLAG + 1
    white = pl.BlockSpec((FBLOCK, depth, rows), lambda g: (jnp.minimum(g, f_steps - 1), 0, 0))
    square = pl.BlockSpec((rows, rows), lambda g: (0, 0))
    specs = [white] * (2 + len(fars)) + [square] * 2 + [pl.BlockSpec(table.shape, lambda g: (0, 0))]
    args = [own1, own2, *fars, recip, keep, table]
    aliases = {}
    if previous is not None:
        aliases = {len(args): 0}
        specs.append(pl.BlockSpec(memory_space=pl.ANY))
        args.append(previous)
    return pl.pallas_call(
        lambda *refs: pair_kernel(f_steps, len(fars), *refs),
        grid=(f_steps + i_steps,),
        in_specs=specs,
        out_specs=pl.BlockSpec(
            (lags, IBLOCK, rows), lambda g: (0, jnp.maximum(g - f_steps, 0), place)
        ),
        out_shape=jax.ShapeDtypeStruct((lags, rows, halves * rows), jnp.bfloat16),
        scratch_shapes=[
            pltpu.VMEM((bins * 2 * rows, rows), jnp.float32),
            pltpu.VMEM((lags * IBLOCK, rows), jnp.float32),
        ],
        input_output_aliases=aliases,
        compiler_params=pltpu.CompilerParams(vmem_limit_bytes=44 * 2**20),
        cost_estimate=pl.CostEstimate(
            flops=8 * bins * rows * rows * (2 * depth + lags) // 2,
            bytes_accessed=bins * depth * rows * 8 + rows * rows * lags * 2,
            transcendentals=0,
        ),
        name="pair_block_%d" % place,
    )(*args)


def direct_body(raw, seg_mask, band):
    rows = raw.shape[0]
    seg_count = raw.shape[1] // (WSEG * W)
    n = lax.axis_size("chan")
    chan_index = lax.axis_index("chan")
    seg_index = lax.axis_index("seg")
    flags = seg_mask.astype(jnp.float32)
    own_flags = lax.dynamic_slice_in_dim(flags, seg_index * seg_count, seg_count, 1)

    def send(value, pairs):
        return lax.ppermute(
            value, ("chan", "seg"), [(a % n * 2 + s, b % n * 2 + t) for a, s, b, t in pairs]
        )

    blocks = range(n)
    near = [b for b in blocks if b % 2 == 0]
    odd = [b for b in blocks if b % 2 == 1]
    y_first = [(b, 0, b + 2, 0) for b in blocks] + [(b, 1, b, 1) for b in blocks]
    y_second = [(b, 1, b + 2, 0) for b in blocks] + [(b, 0, b, 1) for b in blocks]
    x_pairs = [
        [(b, s, b + 1, 0) for b in ups] + [(b, 1 - s, b - 1, 1) for b in downs]
        for ups, downs in ((near, odd), (odd, near))
        for s in range(2)
    ]
    x_flag_pairs = [(b, 0, b + 1, 0) for b in blocks] + [(b, 1, b - 1, 1) for b in blocks]
    white, late_flags = lax.optimization_barrier((whiten(raw, own_flags), flags))
    y_flags = send(late_flags, y_first)
    x_flags = send(late_flags, x_flag_pairs)
    own_other = send(white, [(b, s, b, 1 - s) for b in blocks for s in range(2)])
    y1 = send(white, y_first)
    y2 = send(white, y_second)
    x1 = send(white, x_pairs[0])
    x2 = send(white, x_pairs[1])
    later, own_other, y1, y2, x1, x2, y_flags, x_flags = lax.optimization_barrier(
        (white, own_other, y1, y2, x1, x2, y_flags, x_flags)
    )
    x3 = send(later, x_pairs[2])
    x4 = send(later, x_pairs[3])

    table = lag_table(W, K, MAXLAG).reshape(2 * MAXLAG + 1, 2 * K)
    table = jnp.pad(table, ((0, -table.shape[0] % 16), (0, 0)))
    row_ids = chan_index * rows + jnp.arange(rows, dtype=jnp.int32)

    def factors(far_flags, block):
        counts = WSEG * jnp.sum(flags[:, None, :] * far_flags[None, :, :], axis=-1)
        col_ids = (block * rows + jnp.arange(rows, dtype=jnp.int32)) % C
        diff = (col_ids[None, :] - row_ids[:, None]) % C
        distance = jnp.minimum(diff, C - diff)
        keep = (distance >= band[:, 0:1]) & (distance <= band[:, 1:2])
        return 1.0 / jnp.maximum(counts, 1.0), keep.astype(jnp.float32)

    y_recip, y_keep = factors(y_flags, chan_index - 2 + 2 * seg_index)
    x_recip, x_keep = factors(x_flags, chan_index - 1 + 2 * seg_index)
    out = pair_block(white, own_other, (y1, y2), y_recip, y_keep, table, 0, 2)
    out = pair_block(white, own_other, (x1, x2, x3, x4), x_recip, x_keep, table, 1, 2, out)
    return jnp.transpose(out, (1, 0, 2))


def solution(mesh):
    in_specs = (P(("sub", "chan"), "seg"), P(("sub", "chan"), None), P(("sub", "chan"), None))
    out_specs = P(("sub", "chan"), None, "seg")
    direct = mesh.shape["chan"] == 8 and mesh.shape["seg"] == 2
    body = direct_body if direct else ring_body
    return jax.shard_map(body, mesh=mesh, in_specs=in_specs, out_specs=out_specs, check_vma=False)
```
